256 devices in a mesh: lon: 32 (over x, y, core), bal: 8 (over z).
Axes of the slice: x: 4, y: 4, z: 8, core: 2. Of those that a mesh axis runs over, the one named last changes fastest.
Arguments:
- conc: float32 [524288, 128], P(('lon', 'bal')), may hold values from -6 to 6
- neighbours: int32 [4096, 8], P(('lon', 'bal')), may hold values from 0 to 4095, as said below
- counts: int32 [4096], P(('lon', 'bal')), may hold values from 1 to 8
- weights: int32 [4096, 8], P(('lon', 'bal')), may hold values from 1 to 15
- zones: int32 [524288], P(('lon', 'bal')), may hold values from 0 to 31
- owners: int32 [524288, 1], P(('lon', 'bal')), may hold values from 0 to 7; in each aligned block of 2048 rows (0 to 2047, 2048 to 4095, ...) at most 512 rows name the same one
- rate_table: float32 [32, 128], replicated, may hold values from 0.05 to 1
- reaction: bfloat16 [128, 128], replicated, may hold values from -0.5 to 0.5
Outputs:
- conc_out: bfloat16 [524288, 128], P(('lon', 'bal'))
- chem_slots: bfloat16 [1048576, 128], P(('lon', 'bal'))
The draws below stay inside these ranges and needn't reach their ends.
Inputs may be any that keep to these rules, and one draw needn't show every extreme that they name: neighbours[g, k] is a block of the same bal index as g, on the same longitude band or on the band just before or after it, with the bands wrapping around. On every trajectory owner, at most 512 of its parcels have the same owners value; on some trajectory owners one value is taken exactly 512 times.
All inputs are finite; a program needn't handle non-finite values.
Results may differ from the reference program's by a relative error of at most 0.0085.
Values may be sent and summed in bfloat16 or wider, within the bound.
A program may use at most 64 MiB of HBM per device.

```python
import math
import jax
import jax.numpy as jnp
import numpy as np
from jax import lax

S = 128
BLK = 128
KADJ = 8
ZONES = 32
SUBSTEPS = 12
NB_DEV = 16
P_DEV = 2048
PARCELS = 524288
NBLOCKS = 4096
BAND = 128
CAP = 512
SLOTS = 1048576
N_LON = 32
N_BAL = 8


def draw_neighbours(key, part):
    key_side, key_local = jax.random.split(jax.random.fold_in(key, 17))
    side = jax.random.randint(key_side, (NBLOCKS, KADJ), -1, 2, dtype=jnp.int32)
    local = jax.random.randint(key_local, (NBLOCKS, KADJ), 0, NB_DEV, dtype=jnp.int32)
    block = jnp.arange(NBLOCKS, dtype=jnp.int32)[:, None]
    first = block // NB_DEV * NB_DEV
    return ((first + side * BAND + local + NBLOCKS) % NBLOCKS).astype(jnp.int32)


def set_ends(result, key, least, high):
    shape = result.shape
    place = [jax.random.randint(jax.random.fold_in(key, axis), (), 0, shape[axis]) for axis in range(len(shape))]
    result = result.at[tuple(place)].set(least)
    longest = shape.index(max(shape))
    place[longest] = (place[longest] + 1) % shape[longest]
    return result.at[tuple(place)].set(high)


def levels(own_key, dims, shards, smallest, top_value):
    def one(dim, blocks):
        draws = jax.random.uniform(jax.random.fold_in(jax.random.fold_in(own_key, 6), dim), (blocks,), jnp.float32, smallest / len(shards), top_value / len(shards))
        return jnp.repeat(jnp.exp(draws), dims[dim] // blocks).reshape((-1,) + (1,) * (len(dims) - dim - 1))

    gain = one(*shards[0])
    for cut in shards[1:]:
        gain = gain * one(*cut)
    return gain


def shared_out(stream_key, own, number, rows, number_of, top, limit, lean):
    ranking = jax.random.permutation(stream_key, number_of)
    heavy_load, usual = shares(number_of, rows * top, limit, lean, True), shares(number_of, rows * top, limit, lean, False)
    places = jnp.arange(number_of)

    def named(tallies, turn):
        used = int((tallies > 0).sum())
        fixed = max(1, used // 4)
        moved = fixed + (places - fixed + turn * (used - fixed)) % max(1, number_of - fixed)
        return jnp.zeros((number_of,), jnp.int32).at[ranking[jnp.where(places < fixed, places, moved)]].set(jnp.asarray(tallies, jnp.int32))

    tallies = jnp.where(number % 4 == 0, named(heavy_load, number // 4), named(usual, number - number // 4 - 1))
    mixed = jax.random.permutation(jax.random.fold_in(own, 3), number_of)
    donor, sink = mixed[0:number_of // 2 * 2:2], mixed[1:number_of // 2 * 2:2]
    slack = jnp.minimum(tallies[donor] - 1, limit - tallies[sink]) // 2
    slack = jnp.where((donor == ranking[0]) | (sink == ranking[0]) | (tallies[sink] == 0), 0, jnp.maximum(slack, 0))
    moved = jax.random.randint(jax.random.fold_in(own, 4), (number_of // 2,), 0, 1 << 20) % (slack + 1)
    tallies = tallies.at[donor].add(-moved).at[sink].add(moved)
    labels = jnp.searchsorted(jnp.cumsum(tallies), jnp.arange(rows * top), side="right").astype(jnp.int32)
    table = labels.reshape(top, rows).T
    table = table[jax.random.permutation(jax.random.fold_in(own, 1), rows)]
    turn = jax.random.randint(jax.random.fold_in(own, 2), (rows, 1), 0, top)
    return jnp.take_along_axis(table, (jnp.arange(top)[None, :] + turn) % top, axis=1)


def shares(count, total, limit, slope, full):
    loads = [(1 << 20) // math.isqrt(rank ** slope) + 1 for rank in range(1, count + 1)]
    largest = limit if full else min(limit, max(-(-total // count), total * loads[0] // sum(loads)))
    least = 1 if total - largest >= count - 1 else 0
    given, surplus = [largest] + [least] * (count - 1), total - largest - least * (count - 1)
    while surplus > 0:
        movable = [i for i in range(1, count) if given[i] < largest] or [i for i in range(1, count) if given[i] < limit]
        mass, remaining = sum([loads[i] for i in movable]), surplus
        for i in movable:
            more = min(limit - given[i], max(1, remaining * loads[i] // mass), surplus)
            given[i] = given[i] + more
            surplus = surplus - more
    return np.array(given)


def gaussian(key, dims, deviation, most, pieces=(), kind=jnp.bfloat16):
    drawn = deviation * jax.random.normal(key, dims, jnp.float32)
    if pieces:
        drawn = drawn * levels(key, dims, pieces, -0.22, 0.18)
    return jnp.clip(drawn, -most, most).astype(kind)


def setup_inputs(seed: int = 0) -> dict:
    key_list = jax.random.split(jax.random.key(seed), 9)
    conc = gaussian(key_list[0], (PARCELS, S), 1.0, 6.0, ((0, 256),), jnp.float32)
    neighbours = draw_neighbours(jax.random.fold_in(key_list[8], 71), 0)
    counts = set_ends(jax.random.randint(key_list[2], (NBLOCKS,), 1, KADJ + 1), jax.random.fold_in(key_list[2], 1), 1, KADJ).astype(jnp.int32)
    weights = set_ends(jax.random.randint(key_list[3], (NBLOCKS, KADJ), 1, 16), jax.random.fold_in(key_list[3], 1), 1, 15).astype(jnp.int32)
    zones = set_ends(jax.random.randint(key_list[4], (PARCELS,), 0, ZONES), jax.random.fold_in(key_list[4], 1), 0, ZONES - 1).astype(jnp.int32)
    owners_keys = jax.random.split(jax.random.fold_in(key_list[5], 1), PARCELS // P_DEV)
    owners_turns = jax.random.permutation(jax.random.fold_in(key_list[5], 3), PARCELS // P_DEV)
    owners = jax.vmap(lambda own, number: shared_out(jax.random.fold_in(key_list[5], 2), own, number, P_DEV, N_BAL, 1, CAP, 1))(owners_keys, owners_turns).reshape((PARCELS, 1))
    rate_table = jnp.clip(jnp.exp(jax.random.uniform(key_list[6], (ZONES, S), jnp.float32, math.log(0.05), math.log(1.0))), 0.05, 1.0)
    reaction = gaussian(key_list[7], (S, S), S ** -0.5, 0.5)
    return {"conc": conc, "neighbours": neighbours, "counts": counts, "weights": weights, "zones": zones, "owners": owners, "rate_table": rate_table, "reaction": reaction}


def chemistry(state, reaction):
    def advance(step_index, current):
        tendency = jnp.dot(current.astype(jnp.bfloat16), reaction, preferred_element_type=jnp.float32)
        return current + 0.25 * jnp.tanh(tendency)
    return lax.fori_loop(0, SUBSTEPS, advance, state.astype(jnp.float32)).astype(jnp.bfloat16)


def reference(conc, neighbours, counts, weights, zones, owners, rate_table, reaction):
    blocks = conc.reshape(NBLOCKS, BLK, S)
    mixed = blocks
    outflow = jnp.zeros_like(blocks)
    for column in range(KADJ):
        target = neighbours[:, column]
        coef = jnp.where(column < counts, weights[:, column].astype(jnp.float32) / 128.0, 0.0)
        flux = coef[:, None, None] * (blocks[target] - blocks)
        mixed = mixed + flux
        outflow = outflow.at[target].add(flux)
    mixed = (mixed - outflow).reshape(PARCELS, S)
    photo = mixed * jnp.exp(-rate_table[zones])
    conc_out = chemistry(photo.astype(jnp.bfloat16), reaction)
    devices = N_LON * N_BAL
    owner = owners[:, 0].reshape(devices, P_DEV)
    onehot = (owner[:, :, None] == jnp.arange(N_BAL, dtype=jnp.int32)[None, None, :]).astype(jnp.int32)
    rank = jnp.sum((jnp.cumsum(onehot, axis=1) - onehot) * onehot, axis=2)
    device = jnp.arange(devices, dtype=jnp.int32)[:, None]
    band = device // N_BAL
    source = device % N_BAL
    row = (((band * N_BAL + owner) * N_BAL + source) * CAP + rank).astype(jnp.int32)
    chem_slots = jnp.zeros((SLOTS, S), jnp.bfloat16).at[row.reshape(-1)].set(conc_out)
    return conc_out, chem_slots
```

```python
import functools

import jax
import jax.numpy as jnp
from jax import lax
from jax.experimental import pallas as pl
from jax.experimental.pallas import tpu as pltpu
from jax.sharding import PartitionSpec as P

SUBSTEPS = 12
MESH = pl.DeviceIdType.MESH
F32 = jnp.float32
BF16 = jnp.bfloat16


def dot(a, b):
    return jnp.dot(a, b, preferred_element_type=F32)


def dot_nt(a, b):
    return lax.dot_general(a, b, (((1,), (1,)), ((), ())), preferred_element_type=F32)


def iota(shape, dim):
    return lax.broadcasted_iota(jnp.int32, shape, dim)


def chemistry(start, weights):
    half = start.shape[0] // 2
    width = start.shape[1]
    y = jnp.concatenate([start[:half], start[half:]], axis=1).astype(F32)

    def advance(_, y):
        return y + 0.25 * jnp.tanh(dot(y.astype(BF16), weights))

    y = lax.fori_loop(0, SUBSTEPS, advance, y).astype(BF16)
    return jnp.concatenate([y[:, :width], y[:, width:]], axis=0)


def step_kernel(
    nl, nb, early, conc, near_t, counts, weight_t, zones, owners, rates, reaction, out_conc, out_slots,
    xf, xb, factor, start, result, staged, f_send, f_recv, mix, chem_w,
    load_sem, store_sem, f_sems, halo_sems, slot_sems,
):
    li = lax.axis_index("lon")
    bi = lax.axis_index("bal")
    nblk, blk, width = xf.shape
    kadj = near_t.shape[0]
    nzones = rates.shape[0]
    cap = staged.shape[1]
    rows = nblk * blk
    grp = 16
    left = {"lon": lax.rem(li + nl - 1, nl)}
    right = {"lon": lax.rem(li + 1, nl)}

    def peer(d):
        return {"bal": lax.rem(bi + d, nb)}

    def remote(src, dst, sems, i, device):
        return pltpu.make_async_remote_copy(
            src_ref=src, dst_ref=dst, send_sem=sems.at[0, i], recv_sem=sems.at[1, i],
            device_id=device, device_id_type=MESH,
        )

    load = pltpu.make_async_copy(conc, xf, load_sem)
    load.start()
    barrier = pltpu.get_barrier_semaphore()
    for device in [left, right] + [peer(d) for d in range(1, nb)]:
        pl.semaphore_signal(barrier, inc=1, device_id=device, device_id_type=MESH)

    near = near_t[...]
    band = near // (nblk * nb)
    apart = band - li
    place = jnp.where(
        apart == 0, nblk, jnp.where((apart == 1) | (apart == 1 - nl), 2 * nblk, 0)
    ) + near % nblk
    used = iota((kadj, nblk), 0) < counts[...]
    coef = jnp.where(used, weight_t[...].astype(F32) / 128.0, 0.0)
    which = iota((3 * nblk, nblk), 0)
    ft = jnp.zeros((3 * nblk, nblk), F32)
    for k in range(kadj):
        ft = ft + jnp.where(place[k : k + 1, :] == which, coef[k : k + 1, :], 0.0)
    f_send[...] = jnp.zeros_like(f_send)
    f_send[0, :, :nblk] = ft[:nblk]
    f_send[1, :, :nblk] = ft[2 * nblk :]

    pl.semaphore_wait(barrier, nb + 1)
    to_left = remote(f_send.at[0], f_recv.at[1], f_sems, 0, left)
    to_right = remote(f_send.at[1], f_recv.at[0], f_sems, 1, right)
    to_left.start()
    to_right.start()
    load.wait()
    xb[pl.ds(nblk, nblk)] = xf[...].astype(BF16)
    own_blocks = xb.at[pl.ds(nblk, nblk)]
    halo_left = remote(own_blocks, xb.at[pl.ds(2 * nblk, nblk)], halo_sems, 0, left)
    halo_right = remote(own_blocks, xb.at[pl.ds(0, nblk)], halo_sems, 1, right)
    halo_left.start()
    halo_right.start()

    chem_w[...] = jnp.zeros_like(chem_w)
    chem_w[:width, :width] = reaction[...]
    chem_w[width:, width:] = reaction[...]

    own = owners[...]
    member = jnp.concatenate([(own == o).astype(F32) for o in range(nb)], axis=0)
    member_b = member.astype(BF16)
    before = (iota((blk, blk), 0) < iota((blk, blk), 1)).astype(F32).astype(BF16)
    in_row = dot(member_b, before)
    totals = dot(member_b, jnp.ones((blk, blk), BF16))
    r0, r1 = iota((nb * nblk, nb * nblk), 0), iota((nb * nblk, nb * nblk), 1)
    earlier = ((r0 // nblk == r1 // nblk) & (r1 < r0)).astype(F32).astype(BF16)
    offset = dot(earlier, totals.astype(BF16))
    ranks = (member * (in_row + offset)).reshape(nb, nblk, blk).sum(axis=0)
    slot = own * cap + ranks.astype(jnp.int32)

    table = jnp.exp(-rates[...])
    high = table.astype(BF16)
    rest = table - high.astype(F32)
    mid = rest.astype(BF16)
    low = (rest - mid.astype(F32)).astype(BF16)
    parts = jnp.concatenate([high, mid, low, jnp.zeros_like(low)], axis=0)
    zone_t = zones[...].astype(F32).T.astype(jnp.int32)
    lane = iota((blk, 4 * nzones), 1) % nzones
    for b in range(nblk):
        pick = (zone_t[:, b : b + 1] == lane).astype(F32).astype(BF16)
        factor[b] = dot(pick, parts)

    spread = (iota((nblk * grp, nblk), 0) // grp == iota((nblk * grp, nblk), 1)).astype(F32)
    spread_b = spread.astype(BF16)
    widen = (iota((nblk, nblk * grp), 1) // grp == iota((nblk, nblk * grp), 0)).astype(F32).astype(BF16)
    same = (
        iota((nblk * grp, nblk * grp), 0) % grp == iota((nblk * grp, nblk * grp), 1) % grp
    ).astype(F32)
    ft_b = ft.astype(BF16)
    to_left.wait_recv()
    to_right.wait_recv()
    from_left = f_recv[0, :, :nblk].astype(BF16)
    from_right = f_recv[1, :, :nblk].astype(BF16)
    own_ft = ft_b[nblk : 2 * nblk]
    a_own = (dot(spread_b, own_ft) + dot_nt(spread_b, own_ft)) * (1.0 - spread)
    a_left = dot_nt(spread_b, ft_b[:nblk]) + dot(spread_b, from_left)
    a_right = dot_nt(spread_b, ft_b[2 * nblk :]) + dot(spread_b, from_right)
    keep = 1.0 - jnp.sum(a_own + a_left + a_right, axis=1, keepdims=True)
    for i, a in enumerate((a_left, a_own, a_right)):
        mix[i] = (dot(a.astype(BF16), widen) * same).astype(BF16)

    def group(ref, first, j):
        return ref[pl.ds(first, nblk), pl.ds(pl.multiple_of(j * grp, grp), grp), :].reshape(
            nblk * grp, width
        )

    groups = blk // grp

    def add_own(j, carry):
        at = (pl.ds(0, nblk), pl.ds(pl.multiple_of(j * grp, grp), grp), slice(None))
        mixed = group(xf, 0, j) * keep + dot(mix[1], group(xb, nblk, j))
        xf[at] = mixed.reshape(nblk, grp, width)
        return carry

    lax.fori_loop(0, groups, add_own, 0)
    halo_left.wait_recv()
    halo_right.wait_recv()

    def add_halo(j, carry):
        at = (pl.ds(0, nblk), pl.ds(pl.multiple_of(j * grp, grp), grp), slice(None))
        mixed = (
            group(xf, 0, j)
            + dot(mix[0], group(xb, 0, j))
            + dot(mix[2], group(xb, 2 * nblk, j))
        )
        photo = mixed * group(factor, 0, j)
        start[at] = photo.astype(BF16).reshape(nblk, grp, width)
        return carry

    lax.fori_loop(0, groups, add_halo, 0)

    slot_row = iota((cap, blk), 0)

    def pick_slots(values, d):
        base = lax.rem(bi + d, nb) * cap
        row = slot_row + base
        chosen = jnp.concatenate(
            [(slot[b : b + 1, :] == row).astype(F32).astype(BF16) for b in range(nblk)], axis=1
        )
        return dot(chosen, values).astype(BF16)

    def send(d, i):
        copy = remote(
            staged.at[d], out_slots.at[pl.ds(pl.multiple_of(bi * cap, cap), cap)], slot_sems, i, peer(d)
        )
        copy.start()
        return copy

    order = sorted(range(1, nb), key=lambda d: (-min(d, nb - d), d))
    copies = []
    initial = start[...].reshape(rows, width)
    for d in order[:early]:
        staged[d] = chemistry(pick_slots(initial, d), chem_w[...])
        copies.append(send(d, len(copies)))
    for c in range(4):
        part = rows // 4
        result[pl.ds(c * part, part), :] = chemistry(initial[c * part : (c + 1) * part], chem_w[...])
    final = result[...]
    for d in order[early:]:
        staged[d] = pick_slots(final, d)
        copies.append(send(d, len(copies)))
    save = pltpu.make_async_copy(result, out_conc, store_sem.at[0])
    save.start()
    staged[0] = pick_slots(final, 0)
    keep_own = pltpu.make_async_copy(
        staged.at[0], out_slots.at[pl.ds(pl.multiple_of(bi * cap, cap), cap)], store_sem.at[1]
    )
    keep_own.start()
    for copy in (to_left, to_right, halo_left, halo_right):
        copy.wait_send()
    for copy in copies:
        copy.wait()
    save.wait()
    keep_own.wait()


def solution(mesh):
    nl, nb = mesh.shape["lon"], mesh.shape["bal"]
    early = min(2, nb - 1)

    def shards(conc, neighbours, counts, weights, zones, owners, rate_table, reaction):
        rows, width = conc.shape
        nblk = neighbours.shape[0]
        blk = rows // nblk
        cap = 2 * rows // nb
        vmem = pl.BlockSpec(memory_space=pltpu.VMEM)
        hbm = pl.BlockSpec(memory_space=pltpu.HBM)
        return pl.pallas_call(
            functools.partial(step_kernel, nl, nb, early),
            out_shape=(
                jax.ShapeDtypeStruct((rows, width), BF16),
                jax.ShapeDtypeStruct((nb * cap, width), BF16),
            ),
            in_specs=[hbm] + [vmem] * 7,
            out_specs=(hbm, hbm),
            scratch_shapes=[
                pltpu.VMEM((nblk, blk, width), F32),
                pltpu.VMEM((3 * nblk, blk, width), BF16),
                pltpu.VMEM((nblk, blk, width), F32),
                pltpu.VMEM((nblk, blk, width), BF16),
                pltpu.VMEM((rows, width), BF16),
                pltpu.VMEM((nb, cap, width), BF16),
                pltpu.VMEM((2, nblk, 128), F32),
                pltpu.VMEM((2, nblk, 128), F32),
                pltpu.VMEM((3, nblk * 16, nblk * 16), BF16),
                pltpu.VMEM((2 * width, 2 * width), BF16),
                pltpu.SemaphoreType.DMA,
                pltpu.SemaphoreType.DMA((2,)),
                pltpu.SemaphoreType.DMA((2, 2)),
                pltpu.SemaphoreType.DMA((2, 2)),
                pltpu.SemaphoreType.DMA((2, nb - 1)),
            ],
            compiler_params=pltpu.CompilerParams(
                collective_id=0, has_side_effects=True, vmem_limit_bytes=48 << 20
            ),
        )(
            conc.reshape(nblk, blk, width),
            neighbours.T,
            counts.reshape(1, nblk),
            weights.T,
            zones.reshape(nblk, blk),
            owners.reshape(nblk, blk),
            rate_table,
            reaction,
        )

    in_specs = (
        P(("lon", "bal"), None),
        P(("lon", "bal"), None),
        P(("lon", "bal")),
        P(("lon", "bal"), None),
        P(("lon", "bal")),
        P(("lon", "bal"), None),
        P(),
        P(),
    )
    out_specs = (P(("lon", "bal"), None), P(("lon", "bal"), None))
    return jax.shard_map(shards, mesh=mesh, in_specs=in_specs, out_specs=out_specs, check_vma=False)
```

```python
import functools

import jax
import jax.numpy as jnp
from jax import lax
from jax.experimental import pallas as pl
from jax.experimental.pallas import tpu as pltpu
from jax.sharding import PartitionSpec as P

SUBSTEPS = 12
MESH = pl.DeviceIdType.MESH
F32 = jnp.float32
BF16 = jnp.bfloat16


def dot(a, b):
    return jnp.dot(a, b, preferred_element_type=F32)


def dot_nt(a, b):
    return lax.dot_general(a, b, (((1,), (1,)), ((), ())), preferred_element_type=F32)


def iota(shape, dim):
    return lax.broadcasted_iota(jnp.int32, shape, dim)


def chemistry(start, weights, chain=256):
    rows, width = start.shape
    half = chain // 2
    ys = [
        jnp.concatenate([start[c : c + half], start[c + half : c + chain]], axis=1).astype(F32)
        for c in range(0, rows, chain)
    ]
    for _ in range(SUBSTEPS):
        ys = [y + 0.25 * jnp.tanh(dot(y.astype(BF16), weights)) for y in ys]
    out = []
    for y in ys:
        y = y.astype(BF16)
        out += [y[:, :width], y[:, width:]]
    return jnp.concatenate(out, axis=0)


def step_kernel(
    nl, nb, conc, near_h, counts_h, weight_h, zones_h, owners_h, rates_h, reaction_h, out_conc, out_slots,
    near_t, counts, weight_t, zones, owners, rates, reaction,
    xf, xb, factor, start, result, staged, raw, f_send, f_recv, mix, chem_w,
    load_sem, store_sem, f_sems, halo_sems, slot_sems,
):
    li = lax.axis_index("lon")
    bi = lax.axis_index("bal")
    nblk, blk, width = xf.shape
    kadj = near_t.shape[0]
    nzones = rates.shape[0]
    cap = staged.shape[1]
    rows = nblk * blk
    grp = 16
    left = {"lon": lax.rem(li + nl - 1, nl)}
    right = {"lon": lax.rem(li + 1, nl)}

    def peer(d):
        return {"bal": lax.rem(bi + d, nb)}

    def remote(src, dst, sems, i, device):
        return pltpu.make_async_remote_copy(
            src_ref=src, dst_ref=dst, send_sem=sems.at[0, i], recv_sem=sems.at[1, i],
            device_id=device, device_id_type=MESH,
        )

    small = [
        pltpu.make_async_copy(src, dst, load_sem.at[1 + i])
        for i, (src, dst) in enumerate(
            (
                (near_h, near_t), (counts_h, counts), (weight_h, weight_t), (zones_h, zones),
                (owners_h, owners), (rates_h, rates), (reaction_h, reaction),
            )
        )
    ]
    for copy in small[:3]:
        copy.start()
    load = pltpu.make_async_copy(conc, xf, load_sem.at[0])
    load.start()
    for copy in small[3:]:
        copy.start()
    barrier = pltpu.get_barrier_semaphore()
    for device in [left, right] + [peer(d) for d in range(1, nb)]:
        pl.semaphore_signal(barrier, inc=1, device_id=device, device_id_type=MESH)

    for copy in small[:3]:
        copy.wait()
    near = near_t[...]
    band = near // (nblk * nb)
    apart = band - li
    place = jnp.where(
        apart == 0, nblk, jnp.where((apart == 1) | (apart == 1 - nl), 2 * nblk, 0)
    ) + near % nblk
    used = iota((kadj, nblk), 0) < counts[...]
    coef = jnp.where(used, weight_t[...].astype(F32) / 128.0, 0.0)
    which = iota((3 * nblk, nblk), 0)
    ft = jnp.zeros((3 * nblk, nblk), F32)
    for k in range(kadj):
        ft = ft + jnp.where(place[k : k + 1, :] == which, coef[k : k + 1, :], 0.0)
    f_send[...] = jnp.zeros_like(f_send)
    f_send[0, :, :nblk] = ft[:nblk]
    f_send[1, :, :nblk] = ft[2 * nblk :]

    load.wait()
    xb[pl.ds(nblk, nblk)] = xf[...].astype(BF16)
    own_blocks = xb.at[pl.ds(nblk, nblk)]
    pl.semaphore_wait(barrier, nb + 1)
    to_left = remote(f_send.at[0], f_recv.at[1], f_sems, 0, left)
    to_right = remote(f_send.at[1], f_recv.at[0], f_sems, 1, right)
    to_left.start()
    to_right.start()
    halo_left = remote(own_blocks, xb.at[pl.ds(2 * nblk, nblk)], halo_sems, 0, left)
    halo_right = remote(own_blocks, xb.at[pl.ds(0, nblk)], halo_sems, 1, right)
    halo_left.start()
    halo_right.start()

    for copy in small[3:]:
        copy.wait()
    chem_w[...] = jnp.zeros_like(chem_w)
    chem_w[:width, :width] = reaction[...]
    chem_w[width:, width:] = reaction[...]

    own = owners[...]
    member = jnp.concatenate([(own == o).astype(F32) for o in range(nb)], axis=0)
    member_b = member.astype(BF16)
    before = (iota((blk, blk), 0) < iota((blk, blk), 1)).astype(F32).astype(BF16)
    in_row = dot(member_b, before)
    totals = dot(member_b, jnp.ones((blk, blk), BF16))
    r0, r1 = iota((nb * nblk, nb * nblk), 0), iota((nb * nblk, nb * nblk), 1)
    earlier = ((r0 // nblk == r1 // nblk) & (r1 < r0)).astype(F32).astype(BF16)
    offset = dot(earlier, totals.astype(BF16))
    ranks = (member * (in_row + offset)).reshape(nb, nblk, blk).sum(axis=0)
    slot = own * cap + ranks.astype(jnp.int32)

    table = jnp.exp(-rates[...])
    high = table.astype(BF16)
    rest = table - high.astype(F32)
    mid = rest.astype(BF16)
    low = (rest - mid.astype(F32)).astype(BF16)
    parts = jnp.concatenate([high, mid, low, jnp.zeros_like(low)], axis=0)
    zone_t = zones[...].astype(F32).T.astype(jnp.int32)
    lane = iota((blk, 4 * nzones), 1) % nzones
    for b in range(nblk):
        pick = (zone_t[:, b : b + 1] == lane).astype(F32).astype(BF16)
        factor[b] = dot(pick, parts)

    spread = (iota((nblk * grp, nblk), 0) // grp == iota((nblk * grp, nblk), 1)).astype(F32)
    spread_b = spread.astype(BF16)
    widen = (iota((nblk, nblk * grp), 1) // grp == iota((nblk, nblk * grp), 0)).astype(F32).astype(BF16)
    same = (
        iota((nblk * grp, nblk * grp), 0) % grp == iota((nblk * grp, nblk * grp), 1) % grp
    ).astype(F32)
    ft_b = ft.astype(BF16)
    to_left.wait_recv()
    to_right.wait_recv()
    from_left = f_recv[0, :, :nblk].astype(BF16)
    from_right = f_recv[1, :, :nblk].astype(BF16)
    own_ft = ft_b[nblk : 2 * nblk]
    a_own = (dot(spread_b, own_ft) + dot_nt(spread_b, own_ft)) * (1.0 - spread)
    a_left = dot_nt(spread_b, ft_b[:nblk]) + dot(spread_b, from_left)
    a_right = dot_nt(spread_b, ft_b[2 * nblk :]) + dot(spread_b, from_right)
    keep = 1.0 - jnp.sum(a_own + a_left + a_right, axis=1, keepdims=True)
    mix_own = (dot(a_own.astype(BF16), widen) * same).astype(BF16)
    for i, a in enumerate((a_left, a_right)):
        mix[:, i * nblk * grp : (i + 1) * nblk * grp] = (dot(a.astype(BF16), widen) * same).astype(BF16)

    def pair(ref, first, j):
        parts = [
            ref[first : first + nblk, g * grp : (g + 1) * grp, :].reshape(nblk * grp, width)
            for g in (j, j + 1)
        ]
        return jnp.concatenate(parts, axis=1)

    def put_pair(ref, j, value):
        for g in (j, j + 1):
            part = value[:, (g - j) * width : (g - j + 1) * width]
            ref[:, g * grp : (g + 1) * grp, :] = part.reshape(nblk, grp, width)

    for j in range(0, blk // grp, 2):
        put_pair(xf, j, pair(xf, 0, j) * keep + dot(mix_own, pair(xb, nblk, j)))
    halo_left.wait_recv()
    halo_right.wait_recv()
    for j in range(0, blk // grp, 2):
        halo = jnp.concatenate([pair(xb, 0, j), pair(xb, 2 * nblk, j)], axis=0)
        photo = (pair(xf, 0, j) + dot(mix[...], halo)) * pair(factor, 0, j)
        put_pair(start, j, photo.astype(BF16))

    slot_row = iota((cap, blk), 0)

    def pick_slots(values, d):
        base = lax.rem(bi + d, nb) * cap
        row = slot_row + base
        chosen = jnp.concatenate(
            [(slot[b : b + 1, :] == row).astype(F32).astype(BF16) for b in range(nblk)], axis=1
        )
        return dot(chosen, values).astype(BF16)

    def place_of(d):
        return pl.ds(pl.multiple_of(lax.rem(bi + d, nb) * cap, cap), cap)

    copies = []

    def send(src, dst, d):
        copy = remote(src, dst, slot_sems, len(copies), peer(d))
        copy.start()
        copies.append(copy)

    far = nb // 2
    initial = start[...].reshape(rows, width)
    staged[far] = pick_slots(initial, far)
    send(staged.at[far], raw, far)
    result[...] = chemistry(initial, chem_w[...])
    save = pltpu.make_async_copy(result, out_conc, store_sem.at[0])
    save.start()
    final = result[...]
    for d in sorted(set(range(1, nb)) - {far}, key=lambda d: (-min(d, nb - d), d)):
        staged[d] = pick_slots(final, d)
        send(staged.at[d], out_slots.at[place_of(0)], d)
    staged[0] = pick_slots(final, 0)
    stores = [save, pltpu.make_async_copy(staged.at[0], out_slots.at[place_of(0)], store_sem.at[1])]
    stores[-1].start()
    copies[0].wait()
    staged[far] = chemistry(raw[...], chem_w[...])
    stores.append(pltpu.make_async_copy(staged.at[far], out_slots.at[place_of(nb - far)], store_sem.at[2]))
    stores[-1].start()
    for copy in (to_left, to_right, halo_left, halo_right):
        copy.wait_send()
    for copy in copies[1:] + stores:
        copy.wait()


def solution(mesh):
    nl, nb = mesh.shape["lon"], mesh.shape["bal"]

    def shards(conc, neighbours, counts, weights, zones, owners, rate_table, reaction):
        rows, width = conc.shape
        nblk = neighbours.shape[0]
        blk = rows // nblk
        cap = 2 * rows // nb
        hbm = pl.BlockSpec(memory_space=pltpu.HBM)
        return pl.pallas_call(
            functools.partial(step_kernel, nl, nb),
            out_shape=(
                jax.ShapeDtypeStruct((rows, width), BF16),
                jax.ShapeDtypeStruct((nb * cap, width), BF16),
            ),
            in_specs=[hbm] * 8,
            out_specs=(hbm, hbm),
            scratch_shapes=[
                pltpu.VMEM((neighbours.shape[1], nblk), jnp.int32),
                pltpu.VMEM((1, nblk), jnp.int32),
                pltpu.VMEM((neighbours.shape[1], nblk), jnp.int32),
                pltpu.VMEM((nblk, blk), jnp.int32),
                pltpu.VMEM((nblk, blk), jnp.int32),
                pltpu.VMEM(rate_table.shape, F32),
                pltpu.VMEM(reaction.shape, BF16),
                pltpu.VMEM((nblk, blk, width), F32),
                pltpu.VMEM((3 * nblk, blk, width), BF16),
                pltpu.VMEM((nblk, blk, width), F32),
                pltpu.VMEM((nblk, blk, width), BF16),
                pltpu.VMEM((rows, width), BF16),
                pltpu.VMEM((nb, cap, width), BF16),
                pltpu.VMEM((cap, width), BF16),
                pltpu.VMEM((2, nblk, 128), F32),
                pltpu.VMEM((2, nblk, 128), F32),
                pltpu.VMEM((nblk * 16, 2 * nblk * 16), BF16),
                pltpu.VMEM((2 * width, 2 * width), BF16),
                pltpu.SemaphoreType.DMA((8,)),
                pltpu.SemaphoreType.DMA((3,)),
                pltpu.SemaphoreType.DMA((2, 2)),
                pltpu.SemaphoreType.DMA((2, 2)),
                pltpu.SemaphoreType.DMA((2, nb - 1)),
            ],
            compiler_params=pltpu.CompilerParams(
                collective_id=0, has_side_effects=True, vmem_limit_bytes=48 << 20
            ),
        )(
            conc.reshape(nblk, blk, width),
            neighbours.T,
            counts.reshape(1, nblk),
            weights.T,
            zones.reshape(nblk, blk),
            owners.reshape(nblk, blk),
            rate_table,
            reaction,
        )

    in_specs = (
        P(("lon", "bal"), None),
        P(("lon", "bal"), None),
        P(("lon", "bal")),
        P(("lon", "bal"), None),
        P(("lon", "bal")),
        P(("lon", "bal"), None),
        P(),
        P(),
    )
    out_specs = (P(("lon", "bal"), None), P(("lon", "bal"), None))
    return jax.shard_map(shards, mesh=mesh, in_specs=in_specs, out_specs=out_specs, check_vma=False)
```

```python
import functools

import jax
import jax.numpy as jnp
from jax import lax
from jax.experimental import pallas as pl
from jax.experimental.pallas import tpu as pltpu
from jax.sharding import PartitionSpec as P

SUBSTEPS = 12
MESH = pl.DeviceIdType.MESH
F32 = jnp.float32
BF16 = jnp.bfloat16


def dot(a, b):
    return jnp.dot(a, b, preferred_element_type=F32)


def dot_nt(a, b):
    return lax.dot_general(a, b, (((1,), (1,)), ((), ())), preferred_element_type=F32)


def iota(shape, dim):
    return lax.broadcasted_iota(jnp.int32, shape, dim)


def chemistry(start, weights, chain=256):
    rows, width = start.shape
    half = chain // 2
    ys = [
        jnp.concatenate([start[c : c + half], start[c + half : c + chain]], axis=1).astype(F32)
        for c in range(0, rows, chain)
    ]
    for _ in range(SUBSTEPS):
        ys = [y + 0.25 * jnp.tanh(dot(y.astype(BF16), weights)) for y in ys]
    out = []
    for y in ys:
        y = y.astype(BF16)
        out += [y[:, :width], y[:, width:]]
    return jnp.concatenate(out, axis=0)


def step_kernel(
    nl, nb, conc, near_h, counts_h, weight_h, zones_h, owners_h, rates_h, reaction_h, out_conc, out_slots,
    near_t, counts, weight_t, zones, owners, rates, reaction,
    xf, xb, factor, start, result, staged, raw, f_send, f_recv, mix, chem_w,
    load_sem, store_sem, f_sems, halo_sems, slot_sems,
):
    li = lax.axis_index("lon")
    bi = lax.axis_index("bal")
    nblk, blk, width = xf.shape
    kadj = near_t.shape[0]
    nzones = rates.shape[0]
    cap = staged.shape[1]
    rows = nblk * blk
    grp = 16
    left = {"lon": lax.rem(li + nl - 1, nl)}
    right = {"lon": lax.rem(li + 1, nl)}

    def peer(d):
        return {"bal": lax.rem(bi + d, nb)}

    def remote(src, dst, sems, i, device):
        return pltpu.make_async_remote_copy(
            src_ref=src, dst_ref=dst, send_sem=sems.at[0, i], recv_sem=sems.at[1, i],
            device_id=device, device_id_type=MESH,
        )

    small = [
        pltpu.make_async_copy(src, dst, load_sem.at[1 + i])
        for i, (src, dst) in enumerate(
            (
                (near_h, near_t), (counts_h, counts), (weight_h, weight_t), (zones_h, zones),
                (owners_h, owners), (rates_h, rates), (reaction_h, reaction),
            )
        )
    ]
    for copy in small[:3]:
        copy.start()
    load = pltpu.make_async_copy(conc, xf, load_sem.at[0])
    load.start()
    for copy in small[3:]:
        copy.start()
    barrier = pltpu.get_barrier_semaphore()
    for device in [left, right] + [peer(d) for d in range(1, nb)]:
        pl.semaphore_signal(barrier, inc=1, device_id=device, device_id_type=MESH)

    for copy in small[:3]:
        copy.wait()
    near = near_t[...]
    band = near // (nblk * nb)
    apart = band - li
    place = jnp.where(
        apart == 0, nblk, jnp.where((apart == 1) | (apart == 1 - nl), 2 * nblk, 0)
    ) + near % nblk
    used = iota((kadj, nblk), 0) < counts[...]
    coef = jnp.where(used, weight_t[...].astype(F32) / 128.0, 0.0)
    which = iota((3 * nblk, nblk), 0)
    ft = jnp.zeros((3 * nblk, nblk), F32)
    for k in range(kadj):
        ft = ft + jnp.where(place[k : k + 1, :] == which, coef[k : k + 1, :], 0.0)
    f_send[...] = jnp.zeros_like(f_send)
    f_send[0, :, :nblk] = ft[:nblk]
    f_send[1, :, :nblk] = ft[2 * nblk :]

    load.wait()
    xb[pl.ds(nblk, nblk)] = xf[...].astype(BF16)
    own_blocks = xb.at[pl.ds(nblk, nblk)]
    pl.semaphore_wait(barrier, nb + 1)
    to_left = remote(f_send.at[0], f_recv.at[1], f_sems, 0, left)
    to_right = remote(f_send.at[1], f_recv.at[0], f_sems, 1, right)
    to_left.start()
    to_right.start()
    halo_left = remote(own_blocks, xb.at[pl.ds(2 * nblk, nblk)], halo_sems, 0, left)
    halo_right = remote(own_blocks, xb.at[pl.ds(0, nblk)], halo_sems, 1, right)
    halo_left.start()
    halo_right.start()

    for copy in small[3:]:
        copy.wait()
    chem_w[...] = jnp.zeros_like(chem_w)
    chem_w[:width, :width] = reaction[...]
    chem_w[width:, width:] = reaction[...]

    own = owners[...]
    member = jnp.concatenate([(own == o).astype(F32) for o in range(nb)], axis=0)
    member_b = member.astype(BF16)
    before = (iota((blk, blk), 0) < iota((blk, blk), 1)).astype(F32).astype(BF16)
    in_row = dot(member_b, before)
    totals = dot(member_b, jnp.ones((blk, blk), BF16))
    r0, r1 = iota((nb * nblk, nb * nblk), 0), iota((nb * nblk, nb * nblk), 1)
    earlier = ((r0 // nblk == r1 // nblk) & (r1 < r0)).astype(F32).astype(BF16)
    offset = dot(earlier, totals.astype(BF16))
    ranks = (member * (in_row + offset)).reshape(nb, nblk, blk).sum(axis=0)
    slot = own * cap + ranks.astype(jnp.int32)

    table = jnp.exp(-rates[...])
    high = table.astype(BF16)
    rest = table - high.astype(F32)
    mid = rest.astype(BF16)
    low = (rest - mid.astype(F32)).astype(BF16)
    parts = jnp.concatenate([high, mid, low, jnp.zeros_like(low)], axis=0)
    zone_t = zones[...].astype(F32).T.astype(jnp.int32)
    lane = iota((blk, 4 * nzones), 1) % nzones
    for b in range(nblk):
        pick = (zone_t[:, b : b + 1] == lane).astype(F32).astype(BF16)
        factor[b] = dot(pick, parts)

    spread = (iota((nblk * grp, nblk), 0) // grp == iota((nblk * grp, nblk), 1)).astype(F32)
    spread_b = spread.astype(BF16)
    widen = (iota((nblk, nblk * grp), 1) // grp == iota((nblk, nblk * grp), 0)).astype(F32).astype(BF16)
    same = (
        iota((nblk * grp, nblk * grp), 0) % grp == iota((nblk * grp, nblk * grp), 1) % grp
    ).astype(F32)
    ft_b = ft.astype(BF16)
    to_left.wait_recv()
    to_right.wait_recv()
    from_left = f_recv[0, :, :nblk].astype(BF16)
    from_right = f_recv[1, :, :nblk].astype(BF16)
    own_ft = ft_b[nblk : 2 * nblk]
    a_own = (dot(spread_b, own_ft) + dot_nt(spread_b, own_ft)) * (1.0 - spread)
    a_left = dot_nt(spread_b, ft_b[:nblk]) + dot(spread_b, from_left)
    a_right = dot_nt(spread_b, ft_b[2 * nblk :]) + dot(spread_b, from_right)
    keep = 1.0 - jnp.sum(a_own + a_left + a_right, axis=1, keepdims=True)
    mix_own = (dot(a_own.astype(BF16), widen) * same).astype(BF16)
    for i, a in enumerate((a_left, a_right)):
        mix[:, i * nblk * grp : (i + 1) * nblk * grp] = (dot(a.astype(BF16), widen) * same).astype(BF16)

    def pair(ref, first, j):
        parts = [
            ref[first : first + nblk, g * grp : (g + 1) * grp, :].reshape(nblk * grp, width)
            for g in (j, j + 1)
        ]
        return jnp.concatenate(parts, axis=1)

    def put_pair(ref, j, value):
        for g in (j, j + 1):
            part = value[:, (g - j) * width : (g - j + 1) * width]
            ref[:, g * grp : (g + 1) * grp, :] = part.reshape(nblk, grp, width)

    for j in range(0, blk // grp, 2):
        put_pair(xf, j, pair(xf, 0, j) * keep + dot(mix_own, pair(xb, nblk, j)))
    halo_left.wait_recv()
    halo_right.wait_recv()
    for j in range(0, blk // grp, 2):
        halo = jnp.concatenate([pair(xb, 0, j), pair(xb, 2 * nblk, j)], axis=0)
        photo = (pair(xf, 0, j) + dot(mix[...], halo)) * pair(factor, 0, j)
        put_pair(start, j, photo.astype(BF16))

    slot_row = iota((cap, blk), 0)

    def pick_slots(values, d):
        base = lax.rem(bi + d, nb) * cap
        row = slot_row + base
        chosen = jnp.concatenate(
            [(slot[b : b + 1, :] == row).astype(F32).astype(BF16) for b in range(nblk)], axis=1
        )
        return dot(chosen, values).astype(BF16)

    def place_of(d):
        return pl.ds(pl.multiple_of(lax.rem(bi + d, nb) * cap, cap), cap)

    copies = []

    def send(src, dst, d):
        copy = remote(src, dst, slot_sems, len(copies), peer(d))
        copy.start()
        copies.append(copy)

    far = nb // 2
    initial = start[...].reshape(rows, width)
    staged[far] = pick_slots(initial, far)
    send(staged.at[far], raw, far)
    result[...] = chemistry(initial, chem_w[...])
    save = pltpu.make_async_copy(result, out_conc, store_sem.at[0])
    save.start()
    final = result[...]
    for d in sorted(set(range(1, nb)) - {far}, key=lambda d: (-min(d, nb - d), d)):
        staged[d] = pick_slots(final, d)
        send(staged.at[d], out_slots.at[place_of(0)], d)
    staged[0] = pick_slots(final, 0)
    stores = [save, pltpu.make_async_copy(staged.at[0], out_slots.at[place_of(0)], store_sem.at[1])]
    stores[-1].start()
    copies[0].wait()
    staged[far] = chemistry(raw[...], chem_w[...])
    stores.append(pltpu.make_async_copy(staged.at[far], out_slots.at[place_of(nb - far)], store_sem.at[2]))
    stores[-1].start()
    for copy in (to_left, to_right, halo_left, halo_right):
        copy.wait_send()
    for copy in copies[1:] + stores:
        copy.wait()


def save_kernel(pieces, conc_ref, slots_ref, out_conc, out_slots, sems):
    copies = []
    for src, dst in ((slots_ref, out_slots), (conc_ref, out_conc)):
        part = src.shape[0] // pieces
        for p in range(pieces):
            at = pl.ds(p * part, part)
            copies.append(pltpu.make_async_copy(src.at[at], dst.at[at], sems.at[len(copies)]))
            copies[-1].start()
    for copy in copies:
        copy.wait()


def solution(mesh):
    nl, nb = mesh.shape["lon"], mesh.shape["bal"]

    def shards(conc, neighbours, counts, weights, zones, owners, rate_table, reaction):
        rows, width = conc.shape
        nblk = neighbours.shape[0]
        blk = rows // nblk
        cap = 2 * rows // nb
        hbm = pl.BlockSpec(memory_space=pltpu.HBM)
        out_shape = (
            jax.ShapeDtypeStruct((rows, width), BF16),
            jax.ShapeDtypeStruct((nb * cap, width), BF16),
        )
        params = dict(has_side_effects=True, vmem_limit_bytes=48 << 20)
        done = pl.pallas_call(
            functools.partial(step_kernel, nl, nb),
            out_shape=out_shape,
            in_specs=[hbm] * 8,
            out_specs=(pl.BlockSpec(memory_space=pl.ANY),) * 2,
            scratch_shapes=[
                pltpu.VMEM((neighbours.shape[1], nblk), jnp.int32),
                pltpu.VMEM((1, nblk), jnp.int32),
                pltpu.VMEM((neighbours.shape[1], nblk), jnp.int32),
                pltpu.VMEM((nblk, blk), jnp.int32),
                pltpu.VMEM((nblk, blk), jnp.int32),
                pltpu.VMEM(rate_table.shape, F32),
                pltpu.VMEM(reaction.shape, BF16),
                pltpu.VMEM((nblk, blk, width), F32),
                pltpu.VMEM((3 * nblk, blk, width), BF16),
                pltpu.VMEM((nblk, blk, width), F32),
                pltpu.VMEM((nblk, blk, width), BF16),
                pltpu.VMEM((rows, width), BF16),
                pltpu.VMEM((nb, cap, width), BF16),
                pltpu.VMEM((cap, width), BF16),
                pltpu.VMEM((2, nblk, 128), F32),
                pltpu.VMEM((2, nblk, 128), F32),
                pltpu.VMEM((nblk * 16, 2 * nblk * 16), BF16),
                pltpu.VMEM((2 * width, 2 * width), BF16),
                pltpu.SemaphoreType.DMA((8,)),
                pltpu.SemaphoreType.DMA((3,)),
                pltpu.SemaphoreType.DMA((2, 2)),
                pltpu.SemaphoreType.DMA((2, 2)),
                pltpu.SemaphoreType.DMA((2, nb - 1)),
            ],
            compiler_params=pltpu.CompilerParams(collective_id=0, **params),
        )(
            *(
                pltpu.with_memory_space_constraint(a, pltpu.HBM)
                for a in (
                    conc.reshape(nblk, blk, width),
                    neighbours.T,
                    counts.reshape(1, nblk),
                    weights.T,
                    zones.reshape(nblk, blk),
                    owners.reshape(nblk, blk),
                    rate_table,
                    reaction,
                )
            )
        )
        pieces = 4
        return pl.pallas_call(
            functools.partial(save_kernel, pieces),
            out_shape=out_shape,
            in_specs=[pl.BlockSpec(memory_space=pl.ANY)] * 2,
            out_specs=(hbm, hbm),
            scratch_shapes=[pltpu.SemaphoreType.DMA((2 * pieces,))],
            compiler_params=pltpu.CompilerParams(**params),
        )(*done)

    in_specs = (
        P(("lon", "bal"), None),
        P(("lon", "bal"), None),
        P(("lon", "bal")),
        P(("lon", "bal"), None),
        P(("lon", "bal")),
        P(("lon", "bal"), None),
        P(),
        P(),
    )
    out_specs = (P(("lon", "bal"), None), P(("lon", "bal"), None))
    return jax.shard_map(shards, mesh=mesh, in_specs=in_specs, out_specs=out_specs, check_vma=False)
```

```python
import functools

import jax
import jax.numpy as jnp
from jax import lax
from jax.experimental import pallas as pl
from jax.experimental.pallas import tpu as pltpu
from jax.sharding import PartitionSpec as P

SUBSTEPS = 12
MESH = pl.DeviceIdType.MESH
F32 = jnp.float32
BF16 = jnp.bfloat16


def dot(a, b):
    return jnp.dot(a, b, preferred_element_type=F32)


def dot_nt(a, b):
    return lax.dot_general(a, b, (((1,), (1,)), ((), ())), preferred_element_type=F32)


def iota(shape, dim):
    return lax.broadcasted_iota(jnp.int32, shape, dim)


def chemistry(start, weights, chain=256):
    rows, width = start.shape
    half = chain // 2
    ys = [
        jnp.concatenate([start[c : c + half], start[c + half : c + chain]], axis=1).astype(F32)
        for c in range(0, rows, chain)
    ]
    for _ in range(SUBSTEPS):
        ys = [y + 0.25 * jnp.tanh(dot(y.astype(BF16), weights)) for y in ys]
    out = []
    for y in ys:
        y = y.astype(BF16)
        out += [y[:, :width], y[:, width:]]
    return jnp.concatenate(out, axis=0)


def step_kernel(
    nl, nb, conc, near_h, counts_h, weight_h, zones_h, owners_h, rates_h, reaction_h, out_conc, out_slots,
    near_t, counts, weight_t, zones, owners, rates, reaction,
    xf, xb, factor, start, result, staged, raw, f_send, f_recv, mix, chem_w,
    load_sem, store_sem, f_sems, halo_sems, slot_sems, ready,
):
    li = lax.axis_index("lon")
    bi = lax.axis_index("bal")
    nblk, blk, width = xf.shape
    kadj = near_t.shape[0]
    nzones = rates.shape[0]
    cap = staged.shape[1]
    rows = nblk * blk
    grp = 16
    left = {"lon": lax.rem(li + nl - 1, nl)}
    right = {"lon": lax.rem(li + 1, nl)}

    def remote(src, dst, sems, i, device):
        return pltpu.make_async_remote_copy(
            src_ref=src, dst_ref=dst, send_sem=sems.at[0, i], recv_sem=sems.at[1, i],
            device_id=device, device_id_type=MESH,
        )

    small = [
        pltpu.make_async_copy(src, dst, load_sem.at[1 + i])
        for i, (src, dst) in enumerate(
            (
                (near_h, near_t), (counts_h, counts), (weight_h, weight_t), (zones_h, zones),
                (owners_h, owners), (rates_h, rates), (reaction_h, reaction),
            )
        )
    ]
    for copy in small[:3]:
        copy.start()
    load = pltpu.make_async_copy(conc, xf, load_sem.at[0])
    load.start()
    for copy in small[3:]:
        copy.start()
    barrier = pltpu.get_barrier_semaphore()
    for device in (left, right):
        pl.semaphore_signal(barrier, inc=1, device_id=device, device_id_type=MESH)
    for d in range(1, nb):

        @pl.when(bi + d < nb)
        def _():
            pl.semaphore_signal(barrier, inc=1, device_id={"bal": bi + d}, device_id_type=MESH)


    for copy in small[:3]:
        copy.wait()
    near = near_t[...]
    band = near // (nblk * nb)
    apart = band - li
    place = jnp.where(
        apart == 0, nblk, jnp.where((apart == 1) | (apart == 1 - nl), 2 * nblk, 0)
    ) + near % nblk
    used = iota((kadj, nblk), 0) < counts[...]
    coef = jnp.where(used, weight_t[...].astype(F32) / 128.0, 0.0)
    which = iota((3 * nblk, nblk), 0)
    ft = jnp.zeros((3 * nblk, nblk), F32)
    for k in range(kadj):
        ft = ft + jnp.where(place[k : k + 1, :] == which, coef[k : k + 1, :], 0.0)
    f_send[...] = jnp.zeros_like(f_send)
    f_send[0, :, :nblk] = ft[:nblk]
    f_send[1, :, :nblk] = ft[2 * nblk :]

    load.wait()
    xb[pl.ds(nblk, nblk)] = xf[...].astype(BF16)
    own_blocks = xb.at[pl.ds(nblk, nblk)]
    pl.semaphore_wait(barrier, 2 + bi)
    to_left = remote(f_send.at[0], f_recv.at[1], f_sems, 0, left)
    to_right = remote(f_send.at[1], f_recv.at[0], f_sems, 1, right)
    to_left.start()
    to_right.start()
    halo_left = remote(own_blocks, xb.at[pl.ds(2 * nblk, nblk)], halo_sems, 0, left)
    halo_right = remote(own_blocks, xb.at[pl.ds(0, nblk)], halo_sems, 1, right)
    halo_left.start()
    halo_right.start()
    for d in range(1, nb):

        @pl.when(bi - d >= 0)
        def _():
            pl.semaphore_signal(ready, inc=1, device_id={"bal": bi - d}, device_id_type=MESH)

    for copy in small[3:]:
        copy.wait()
    chem_w[...] = jnp.zeros_like(chem_w)
    chem_w[:width, :width] = reaction[...]
    chem_w[width:, width:] = reaction[...]

    own = owners[...]
    member = jnp.concatenate([(own == o).astype(F32) for o in range(nb)], axis=0)
    member_b = member.astype(BF16)
    before = (iota((blk, blk), 0) < iota((blk, blk), 1)).astype(F32).astype(BF16)
    in_row = dot(member_b, before)
    totals = dot(member_b, jnp.ones((blk, blk), BF16))
    r0, r1 = iota((nb * nblk, nb * nblk), 0), iota((nb * nblk, nb * nblk), 1)
    earlier = ((r0 // nblk == r1 // nblk) & (r1 < r0)).astype(F32).astype(BF16)
    offset = dot(earlier, totals.astype(BF16))
    ranks = (member * (in_row + offset)).reshape(nb, nblk, blk).sum(axis=0)
    slot = own * cap + ranks.astype(jnp.int32)

    table = jnp.exp(-rates[...])
    high = table.astype(BF16)
    rest = table - high.astype(F32)
    mid = rest.astype(BF16)
    low = (rest - mid.astype(F32)).astype(BF16)
    parts = jnp.concatenate([high, mid, low, jnp.zeros_like(low)], axis=0)
    zone_t = zones[...].astype(F32).T.astype(jnp.int32)
    lane = iota((blk, 4 * nzones), 1) % nzones
    for b in range(nblk):
        pick = (zone_t[:, b : b + 1] == lane).astype(F32).astype(BF16)
        factor[b] = dot(pick, parts)

    spread = (iota((nblk * grp, nblk), 0) // grp == iota((nblk * grp, nblk), 1)).astype(F32)
    spread_b = spread.astype(BF16)
    widen = (iota((nblk, nblk * grp), 1) // grp == iota((nblk, nblk * grp), 0)).astype(F32).astype(BF16)
    same = (
        iota((nblk * grp, nblk * grp), 0) % grp == iota((nblk * grp, nblk * grp), 1) % grp
    ).astype(F32)
    ft_b = ft.astype(BF16)
    to_left.wait_recv()
    to_right.wait_recv()
    from_left = f_recv[0, :, :nblk].astype(BF16)
    from_right = f_recv[1, :, :nblk].astype(BF16)
    own_ft = ft_b[nblk : 2 * nblk]
    a_own = (dot(spread_b, own_ft) + dot_nt(spread_b, own_ft)) * (1.0 - spread)
    a_left = dot_nt(spread_b, ft_b[:nblk]) + dot(spread_b, from_left)
    a_right = dot_nt(spread_b, ft_b[2 * nblk :]) + dot(spread_b, from_right)
    keep = 1.0 - jnp.sum(a_own + a_left + a_right, axis=1, keepdims=True)
    mix_own = (dot(a_own.astype(BF16), widen) * same).astype(BF16)
    for i, a in enumerate((a_left, a_right)):
        mix[:, i * nblk * grp : (i + 1) * nblk * grp] = (dot(a.astype(BF16), widen) * same).astype(BF16)

    def pair(ref, first, j):
        parts = [
            ref[first : first + nblk, g * grp : (g + 1) * grp, :].reshape(nblk * grp, width)
            for g in (j, j + 1)
        ]
        return jnp.concatenate(parts, axis=1)

    def put_pair(ref, j, value):
        for g in (j, j + 1):
            part = value[:, (g - j) * width : (g - j + 1) * width]
            ref[:, g * grp : (g + 1) * grp, :] = part.reshape(nblk, grp, width)

    for j in range(0, blk // grp, 2):
        put_pair(xf, j, pair(xf, 0, j) * keep + dot(mix_own, pair(xb, nblk, j)))
    halo_left.wait_recv()
    halo_right.wait_recv()
    for j in range(0, blk // grp, 2):
        halo = jnp.concatenate([pair(xb, 0, j), pair(xb, 2 * nblk, j)], axis=0)
        photo = (pair(xf, 0, j) + dot(mix[...], halo)) * pair(factor, 0, j)
        put_pair(start, j, photo.astype(BF16))

    slot_row = iota((cap, blk), 0)

    def pick_slots(values, owner):
        row = slot_row + owner * cap
        chosen = jnp.concatenate(
            [(slot[b : b + 1, :] == row).astype(F32).astype(BF16) for b in range(nblk)], axis=1
        )
        return dot(chosen, values).astype(BF16)

    def slots_from(source):
        return out_slots.at[pl.ds(pl.multiple_of(source * cap, cap), cap)]

    copies = []

    def send(src, dst, owner):
        copy = remote(src, dst, slot_sems, len(copies), {"bal": owner})
        copy.start()
        copies.append(copy)

    half = nb // 2
    side, place_in = bi // half, lax.rem(bi, half)
    across = [(1 - side) * half + lax.rem(place_in + k, half) for k in range(half)]
    within = [side * half + lax.rem(place_in + k, half) for k in range(1, half)]

    initial = start[...].reshape(rows, width)
    staged[1] = pick_slots(initial, across[0])

    @pl.when(bi < nb - 1)
    def _():
        pl.semaphore_wait(ready, nb - 1 - bi)

    send(staged.at[1], raw, across[0])
    result[...] = chemistry(initial, chem_w[...])
    save = pltpu.make_async_copy(result, out_conc, store_sem.at[0])
    save.start()
    final = result[...]
    for k, owner in enumerate(across[1:] + within):
        staged[2 + k] = pick_slots(final, owner)
        send(staged.at[2 + k], slots_from(bi), owner)
    staged[0] = pick_slots(final, bi)
    stores = [save, pltpu.make_async_copy(staged.at[0], slots_from(bi), store_sem.at[1])]
    stores[-1].start()
    copies[0].wait()
    staged[1] = chemistry(raw[...], chem_w[...])
    stores.append(pltpu.make_async_copy(staged.at[1], slots_from(across[0]), store_sem.at[2]))
    stores[-1].start()
    for copy in (to_left, to_right, halo_left, halo_right):
        copy.wait_send()
    for copy in copies[1:] + stores:
        copy.wait()


def save_kernel(pieces, conc_ref, slots_ref, out_conc, out_slots, sems):
    copies = []
    for src, dst in ((slots_ref, out_slots), (conc_ref, out_conc)):
        part = src.shape[0] // pieces
        for p in range(pieces):
            at = pl.ds(p * part, part)
            copies.append(pltpu.make_async_copy(src.at[at], dst.at[at], sems.at[len(copies)]))
            copies[-1].start()
    for copy in copies:
        copy.wait()


def solution(mesh):
    nl, nb = mesh.shape["lon"], mesh.shape["bal"]

    def shards(conc, neighbours, counts, weights, zones, owners, rate_table, reaction):
        rows, width = conc.shape
        nblk = neighbours.shape[0]
        blk = rows // nblk
        cap = 2 * rows // nb
        hbm = pl.BlockSpec(memory_space=pltpu.HBM)
        out_shape = (
            jax.ShapeDtypeStruct((rows, width), BF16),
            jax.ShapeDtypeStruct((nb * cap, width), BF16),
        )
        params = dict(has_side_effects=True, vmem_limit_bytes=48 << 20)
        done = pl.pallas_call(
            functools.partial(step_kernel, nl, nb),
            out_shape=out_shape,
            in_specs=[hbm] * 8,
            out_specs=(pl.BlockSpec(memory_space=pl.ANY),) * 2,
            scratch_shapes=[
                pltpu.VMEM((neighbours.shape[1], nblk), jnp.int32),
                pltpu.VMEM((1, nblk), jnp.int32),
                pltpu.VMEM((neighbours.shape[1], nblk), jnp.int32),
                pltpu.VMEM((nblk, blk), jnp.int32),
                pltpu.VMEM((nblk, blk), jnp.int32),
                pltpu.VMEM(rate_table.shape, F32),
                pltpu.VMEM(reaction.shape, BF16),
                pltpu.VMEM((nblk, blk, width), F32),
                pltpu.VMEM((3 * nblk, blk, width), BF16),
                pltpu.VMEM((nblk, blk, width), F32),
                pltpu.VMEM((nblk, blk, width), BF16),
                pltpu.VMEM((rows, width), BF16),
                pltpu.VMEM((nb, cap, width), BF16),
                pltpu.VMEM((cap, width), BF16),
                pltpu.VMEM((2, nblk, 128), F32),
                pltpu.VMEM((2, nblk, 128), F32),
                pltpu.VMEM((nblk * 16, 2 * nblk * 16), BF16),
                pltpu.VMEM((2 * width, 2 * width), BF16),
                pltpu.SemaphoreType.DMA((8,)),
                pltpu.SemaphoreType.DMA((3,)),
                pltpu.SemaphoreType.DMA((2, 2)),
                pltpu.SemaphoreType.DMA((2, 2)),
                pltpu.SemaphoreType.DMA((2, nb - 1)),
                pltpu.SemaphoreType.REGULAR,
            ],
            compiler_params=pltpu.CompilerParams(collective_id=0, **params),
        )(
            *(
                pltpu.with_memory_space_constraint(a, pltpu.HBM)
                for a in (
                    conc.reshape(nblk, blk, width),
                    neighbours.T,
                    counts.reshape(1, nblk),
                    weights.T,
                    zones.reshape(nblk, blk),
                    owners.reshape(nblk, blk),
                    rate_table,
                    reaction,
                )
            )
        )
        pieces = 4
        return pl.pallas_call(
            functools.partial(save_kernel, pieces),
            out_shape=out_shape,
            in_specs=[pl.BlockSpec(memory_space=pl.ANY)] * 2,
            out_specs=(hbm, hbm),
            scratch_shapes=[pltpu.SemaphoreType.DMA((2 * pieces,))],
            compiler_params=pltpu.CompilerParams(**params),
        )(*done)

    in_specs = (
        P(("lon", "bal"), None),
        P(("lon", "bal"), None),
        P(("lon", "bal")),
        P(("lon", "bal"), None),
        P(("lon", "bal")),
        P(("lon", "bal"), None),
        P(),
        P(),
    )
    out_specs = (P(("lon", "bal"), None), P(("lon", "bal"), None))
    return jax.shard_map(shards, mesh=mesh, in_specs=in_specs, out_specs=out_specs, check_vma=False)
```

```python
import functools

import jax
import jax.numpy as jnp
from jax import lax
from jax.experimental import pallas as pl
from jax.experimental.pallas import tpu as pltpu
from jax.sharding import PartitionSpec as P

SUBSTEPS = 12
MESH = pl.DeviceIdType.MESH
F32 = jnp.float32
BF16 = jnp.bfloat16


def dot(a, b):
    return jnp.dot(a, b, preferred_element_type=F32)


def dot_nt(a, b):
    return lax.dot_general(a, b, (((1,), (1,)), ((), ())), preferred_element_type=F32)


def iota(shape, dim):
    return lax.broadcasted_iota(jnp.int32, shape, dim)


def chemistry(start, weights, chain=256):
    rows, width = start.shape
    half = chain // 2
    ys = [
        jnp.concatenate([start[c : c + half], start[c + half : c + chain]], axis=1).astype(F32)
        for c in range(0, rows, chain)
    ]
    for _ in range(SUBSTEPS):
        ys = [y + 0.25 * jnp.tanh(dot(y.astype(BF16), weights)) for y in ys]
    out = []
    for y in ys:
        y = y.astype(BF16)
        out += [y[:, :width], y[:, width:]]
    return jnp.concatenate(out, axis=0)


def cross(first, second):
    half = first.shape[-1] // 2
    low = iota(first.shape, first.ndim - 1) < half

    def turn(v):
        return pltpu.roll(v, half, v.ndim - 1)

    return jnp.where(low, first, turn(second)), jnp.where(low, turn(first), second)


def step_kernel(
    nl, nb, conc, near_h, counts_h, weight_h, zones_h, owners_h, rates_h, reaction_h, out_conc, out_slots,
    near_t, counts, weight_t, zones, owners, rates, reaction,
    xf, xp, xb, factor, start, result, staged, ahead, raw, f_send, f_recv, mix, chem_w,
    load_sem, store_sem, f_sems, halo_sems, slot_sems, ready,
):
    li = lax.axis_index("lon")
    bi = lax.axis_index("bal")
    nblk, blk, width = xf.shape
    kadj = near_t.shape[0]
    nzones = rates.shape[0]
    cap = staged.shape[1]
    rows = nblk * blk
    grp = 16
    hb = blk // 2
    left = {"lon": lax.rem(li + nl - 1, nl)}
    right = {"lon": lax.rem(li + 1, nl)}

    def remote(src, dst, sems, i, device):
        return pltpu.make_async_remote_copy(
            src_ref=src, dst_ref=dst, send_sem=sems.at[0, i], recv_sem=sems.at[1, i],
            device_id=device, device_id_type=MESH,
        )

    small = [
        pltpu.make_async_copy(src, dst, load_sem.at[1 + i])
        for i, (src, dst) in enumerate(
            (
                (near_h, near_t), (counts_h, counts), (weight_h, weight_t), (zones_h, zones),
                (owners_h, owners), (rates_h, rates), (reaction_h, reaction),
            )
        )
    ]
    for copy in small[:3]:
        copy.start()
    load = pltpu.make_async_copy(conc, xf, load_sem.at[0])
    load.start()
    for copy in small[3:]:
        copy.start()
    barrier = pltpu.get_barrier_semaphore()
    for device in (left, right):
        pl.semaphore_signal(barrier, inc=1, device_id=device, device_id_type=MESH)
    for d in range(1, nb):

        @pl.when(bi + d < nb)
        def _():
            pl.semaphore_signal(barrier, inc=1, device_id={"bal": bi + d}, device_id_type=MESH)


    for copy in small[:3]:
        copy.wait()
    near = near_t[...]
    band = near // (nblk * nb)
    apart = band - li
    place = jnp.where(
        apart == 0, nblk, jnp.where((apart == 1) | (apart == 1 - nl), 2 * nblk, 0)
    ) + near % nblk
    used = iota((kadj, nblk), 0) < counts[...]
    coef = jnp.where(used, weight_t[...].astype(F32) / 128.0, 0.0)
    which = iota((3 * nblk, nblk), 0)
    ft = jnp.zeros((3 * nblk, nblk), F32)
    for k in range(kadj):
        ft = ft + jnp.where(place[k : k + 1, :] == which, coef[k : k + 1, :], 0.0)
    f_send[...] = jnp.zeros_like(f_send)
    f_send[0, :, :nblk] = ft[:nblk]
    f_send[1, :, :nblk] = ft[2 * nblk :]

    load.wait()
    for h, packed in enumerate(cross(xf[:, :hb, :], xf[:, hb:, :])):
        xp[h] = packed
        xb[h, nblk : 2 * nblk] = packed.astype(BF16)
    pl.semaphore_wait(barrier, 2 + bi)
    to_left = remote(f_send.at[0], f_recv.at[1], f_sems, 0, left)
    to_right = remote(f_send.at[1], f_recv.at[0], f_sems, 1, right)
    to_left.start()
    to_right.start()
    halos = []
    for h in range(2):
        own_blocks = xb.at[h, pl.ds(nblk, nblk)]
        pair_of = (
            remote(own_blocks, xb.at[h, pl.ds(2 * nblk, nblk)], halo_sems, 2 * h, left),
            remote(own_blocks, xb.at[h, pl.ds(0, nblk)], halo_sems, 2 * h + 1, right),
        )
        for copy in pair_of:
            copy.start()
        halos.append(pair_of)

    for d in range(1, nb):

        @pl.when(bi - d >= 0)
        def _():
            pl.semaphore_signal(ready, inc=1, device_id={"bal": bi - d}, device_id_type=MESH)

    for copy in small[3:]:
        copy.wait()
    chem_w[...] = jnp.zeros_like(chem_w)
    chem_w[:width, :width] = reaction[...]
    chem_w[width:, width:] = reaction[...]

    own = owners[...]
    member = jnp.concatenate([(own == o).astype(F32) for o in range(nb)], axis=0)
    member_b = member.astype(BF16)
    before = (iota((blk, blk), 0) < iota((blk, blk), 1)).astype(F32).astype(BF16)
    in_row = dot(member_b, before)
    totals = dot(member_b, jnp.ones((blk, blk), BF16))
    r0, r1 = iota((nb * nblk, nb * nblk), 0), iota((nb * nblk, nb * nblk), 1)
    earlier = ((r0 // nblk == r1 // nblk) & (r1 < r0)).astype(F32).astype(BF16)
    offset = dot(earlier, totals.astype(BF16))
    ranks = (member * (in_row + offset)).reshape(nb, nblk, blk).sum(axis=0)
    slot = own * cap + ranks.astype(jnp.int32)

    table = jnp.exp(-rates[...])
    high = table.astype(BF16)
    rest = table - high.astype(F32)
    mid = rest.astype(BF16)
    low = (rest - mid.astype(F32)).astype(BF16)
    parts = jnp.concatenate([high, mid, low, jnp.zeros_like(low)], axis=0)
    zone_t = zones[...].astype(F32).T.astype(jnp.int32)
    lane = iota((blk, 4 * nzones), 1) % nzones
    for b in range(nblk):
        pick = (zone_t[:, b : b + 1] == lane).astype(F32).astype(BF16)
        rate = dot(pick, parts)
        for h, packed in enumerate(cross(rate[:hb], rate[hb:])):
            factor[h, b] = packed

    spread = (iota((nblk * grp, nblk), 0) // grp == iota((nblk * grp, nblk), 1)).astype(F32)
    spread_b = spread.astype(BF16)
    widen = (iota((nblk, nblk * grp), 1) // grp == iota((nblk, nblk * grp), 0)).astype(F32).astype(BF16)
    same = (
        iota((nblk * grp, nblk * grp), 0) % grp == iota((nblk * grp, nblk * grp), 1) % grp
    ).astype(F32)
    ft_b = ft.astype(BF16)
    to_left.wait_recv()
    to_right.wait_recv()
    from_left = f_recv[0, :, :nblk].astype(BF16)
    from_right = f_recv[1, :, :nblk].astype(BF16)
    own_ft = ft_b[nblk : 2 * nblk]
    a_own = (dot(spread_b, own_ft) + dot_nt(spread_b, own_ft)) * (1.0 - spread)
    a_left = dot_nt(spread_b, ft_b[:nblk]) + dot(spread_b, from_left)
    a_right = dot_nt(spread_b, ft_b[2 * nblk :]) + dot(spread_b, from_right)
    keep = 1.0 - jnp.sum(a_own + a_left + a_right, axis=1, keepdims=True)
    mix_own = (dot(a_own.astype(BF16), widen) * same).astype(BF16)
    for i, a in enumerate((a_left, a_right)):
        mix[:, i * nblk * grp : (i + 1) * nblk * grp] = (dot(a.astype(BF16), widen) * same).astype(BF16)

    def pair(ref, first, j):
        parts = [
            ref[first : first + nblk, g * grp : (g + 1) * grp, :].reshape(nblk * grp, width)
            for g in (j, j + 1)
        ]
        return jnp.concatenate(parts, axis=1)

    def put_pair(ref, j, value):
        for g in (j, j + 1):
            part = value[:, (g - j) * width : (g - j + 1) * width]
            ref[:, g * grp : (g + 1) * grp, :] = part.reshape(nblk, grp, width)

    for h in range(2):
        for j in range(0, hb // grp, 2):
            own_x = xp.at[h]
            put_pair(own_x, j, pair(own_x, 0, j) * keep + dot(mix_own, pair(xb.at[h], nblk, j)))

    slot_row = iota((cap, blk), 0)

    def choose(owner):
        row = slot_row + owner * cap
        return jnp.concatenate(
            [(slot[b : b + 1, :] == row).astype(F32).astype(BF16) for b in range(nblk)], axis=1
        )

    def pick_slots(values, owner):
        return dot(choose(owner), values).astype(BF16)

    def finish(h):
        for copy in halos[h]:
            copy.wait_recv()
        for j in range(0, hb // grp, 2):
            halo = jnp.concatenate([pair(xb.at[h], 0, j), pair(xb.at[h], 2 * nblk, j)], axis=0)
            photo = (pair(xp.at[h], 0, j) + dot(mix[...], halo)) * pair(factor.at[h], 0, j)
            put_pair(xp.at[h], j, photo.astype(BF16).astype(F32))

    def slots_from(source):
        return out_slots.at[pl.ds(pl.multiple_of(source * cap, cap), cap)]

    copies = []

    def send(src, dst, owner):
        copy = remote(src, dst, slot_sems, len(copies), {"bal": owner})
        copy.start()
        copies.append(copy)

    half = nb // 2
    side, place_in = bi // half, lax.rem(bi, half)
    across = [(1 - side) * half + lax.rem(place_in + k, half) for k in range(half)]
    within = [side * half + lax.rem(place_in + k, half) for k in range(1, half)]

    chosen = choose(across[0])
    finish(0)
    start[:, :hb, :], start[:, hb:, :] = (v.astype(BF16) for v in cross(xp[0], xp[0]))
    rows_low = dot(chosen, start[...].reshape(rows, width))
    ahead[0] = cross(rows_low[: cap // 2], rows_low[cap // 2 :])[0].astype(BF16)

    @pl.when(bi < nb - 1)
    def _():
        pl.semaphore_wait(ready, nb - 1 - bi)

    send(ahead.at[0], raw.at[0], across[0])
    finish(1)
    start[:, :hb, :], start[:, hb:, :] = (v.astype(BF16) for v in cross(xp[0], xp[1]))
    initial = start[...].reshape(rows, width)
    rows_all = dot(chosen, initial)
    ahead[1] = cross(rows_all[: cap // 2], rows_all[cap // 2 :])[1].astype(BF16)
    send(ahead.at[1], raw.at[1], across[0])
    result[...] = chemistry(initial, chem_w[...])
    save = pltpu.make_async_copy(result, out_conc, store_sem.at[0])
    save.start()
    final = result[...]
    for k, owner in enumerate(across[1:] + within):
        staged[2 + k] = pick_slots(final, owner)
        send(staged.at[2 + k], slots_from(bi), owner)
    staged[0] = pick_slots(final, bi)
    stores = [save, pltpu.make_async_copy(staged.at[0], slots_from(bi), store_sem.at[1])]
    stores[-1].start()
    for copy in copies[:2]:
        copy.wait()
    arrived = jnp.concatenate(cross(raw[0].astype(F32), raw[1].astype(F32)), axis=0).astype(BF16)
    staged[1] = chemistry(arrived, chem_w[...])
    stores.append(pltpu.make_async_copy(staged.at[1], slots_from(across[0]), store_sem.at[2]))
    stores[-1].start()
    for copy in (to_left, to_right) + halos[0] + halos[1]:
        copy.wait_send()
    for copy in copies[2:] + stores:
        copy.wait()


def save_kernel(pieces, conc_ref, slots_ref, out_conc, out_slots, sems):
    copies = []
    for src, dst in ((slots_ref, out_slots), (conc_ref, out_conc)):
        part = src.shape[0] // pieces
        for p in range(pieces):
            at = pl.ds(p * part, part)
            copies.append(pltpu.make_async_copy(src.at[at], dst.at[at], sems.at[len(copies)]))
            copies[-1].start()
    for copy in copies:
        copy.wait()


def solution(mesh):
    nl, nb = mesh.shape["lon"], mesh.shape["bal"]

    def shards(conc, neighbours, counts, weights, zones, owners, rate_table, reaction):
        rows, width = conc.shape
        nblk = neighbours.shape[0]
        blk = rows // nblk
        cap = 2 * rows // nb
        hbm = pl.BlockSpec(memory_space=pltpu.HBM)
        out_shape = (
            jax.ShapeDtypeStruct((rows, width), BF16),
            jax.ShapeDtypeStruct((nb * cap, width), BF16),
        )
        params = dict(has_side_effects=True, vmem_limit_bytes=48 << 20)
        done = pl.pallas_call(
            functools.partial(step_kernel, nl, nb),
            out_shape=out_shape,
            in_specs=[hbm] * 8,
            out_specs=(pl.BlockSpec(memory_space=pl.ANY),) * 2,
            scratch_shapes=[
                pltpu.VMEM((neighbours.shape[1], nblk), jnp.int32),
                pltpu.VMEM((1, nblk), jnp.int32),
                pltpu.VMEM((neighbours.shape[1], nblk), jnp.int32),
                pltpu.VMEM((nblk, blk), jnp.int32),
                pltpu.VMEM((nblk, blk), jnp.int32),
                pltpu.VMEM(rate_table.shape, F32),
                pltpu.VMEM(reaction.shape, BF16),
                pltpu.VMEM((nblk, blk, width), F32),
                pltpu.VMEM((2, nblk, blk // 2, width), F32),
                pltpu.VMEM((2, 3 * nblk, blk // 2, width), BF16),
                pltpu.VMEM((2, nblk, blk // 2, width), F32),
                pltpu.VMEM((nblk, blk, width), BF16),
                pltpu.VMEM((rows, width), BF16),
                pltpu.VMEM((nb, cap, width), BF16),
                pltpu.VMEM((2, cap // 2, width), BF16),
                pltpu.VMEM((2, cap // 2, width), BF16),
                pltpu.VMEM((2, nblk, 128), F32),
                pltpu.VMEM((2, nblk, 128), F32),
                pltpu.VMEM((nblk * 16, 2 * nblk * 16), BF16),
                pltpu.VMEM((2 * width, 2 * width), BF16),
                pltpu.SemaphoreType.DMA((8,)),
                pltpu.SemaphoreType.DMA((3,)),
                pltpu.SemaphoreType.DMA((2, 2)),
                pltpu.SemaphoreType.DMA((2, 4)),
                pltpu.SemaphoreType.DMA((2, nb)),
                pltpu.SemaphoreType.REGULAR,
            ],
            compiler_params=pltpu.CompilerParams(collective_id=0, **params),
        )(
            *(
                pltpu.with_memory_space_constraint(a, pltpu.HBM)
                for a in (
                    conc.reshape(nblk, blk, width),
                    neighbours.T,
                    counts.reshape(1, nblk),
                    weights.T,
                    zones.reshape(nblk, blk),
                    owners.reshape(nblk, blk),
                    rate_table,
                    reaction,
                )
            )
        )
        pieces = 4
        return pl.pallas_call(
            functools.partial(save_kernel, pieces),
            out_shape=out_shape,
            in_specs=[pl.BlockSpec(memory_space=pl.ANY)] * 2,
            out_specs=(hbm, hbm),
            scratch_shapes=[pltpu.SemaphoreType.DMA((2 * pieces,))],
            compiler_params=pltpu.CompilerParams(**params),
        )(*done)

    in_specs = (
        P(("lon", "bal"), None),
        P(("lon", "bal"), None),
        P(("lon", "bal")),
        P(("lon", "bal"), None),
        P(("lon", "bal")),
        P(("lon", "bal"), None),
        P(),
        P(),
    )
    out_specs = (P(("lon", "bal"), None), P(("lon", "bal"), None))
    return jax.shard_map(shards, mesh=mesh, in_specs=in_specs, out_specs=out_specs, check_vma=False)
```

```python
import functools

import jax
import jax.numpy as jnp
from jax import lax
from jax.experimental import pallas as pl
from jax.experimental.pallas import tpu as pltpu
from jax.sharding import PartitionSpec as P

SUBSTEPS = 12
MESH = pl.DeviceIdType.MESH
F32 = jnp.float32
BF16 = jnp.bfloat16


def dot(a, b):
    return jnp.dot(a, b, preferred_element_type=F32)


def dot_nt(a, b):
    return lax.dot_general(a, b, (((1,), (1,)), ((), ())), preferred_element_type=F32)


def iota(shape, dim):
    return lax.broadcasted_iota(jnp.int32, shape, dim)


def chemistry(start, weights, chain=256):
    rows, width = start.shape
    half = chain // 2
    ys = [
        jnp.concatenate([start[c : c + half], start[c + half : c + chain]], axis=1).astype(F32)
        for c in range(0, rows, chain)
    ]
    for _ in range(SUBSTEPS):
        ys = [y + 0.25 * jnp.tanh(dot(y.astype(BF16), weights)) for y in ys]
    out = []
    for y in ys:
        y = y.astype(BF16)
        out += [y[:, :width], y[:, width:]]
    return jnp.concatenate(out, axis=0)


def cross(first, second):
    half = first.shape[-1] // 2
    low = iota(first.shape, first.ndim - 1) < half

    def turn(v):
        return pltpu.roll(v, half, v.ndim - 1)

    return jnp.where(low, first, turn(second)), jnp.where(low, turn(first), second)


def step_kernel(
    nl, nb, conc, near_h, counts_h, weight_h, zones_h, owners_h, rates_h, reaction_h, out_conc, out_slots,
    near_t, counts, weight_t, zones, owners, rates, reaction,
    xf, xp, xb, factor, start, result, staged, ahead, raw, f_send, f_recv, mix, chem_w,
    load_sem, store_sem, f_sems, halo_sems, slot_sems, ready,
):
    li = lax.axis_index("lon")
    bi = lax.axis_index("bal")
    nblk, blk, width = xf.shape
    kadj = near_t.shape[0]
    nzones = rates.shape[0]
    cap = staged.shape[1]
    rows = nblk * blk
    grp = 16
    hb = blk // 2
    left = {"lon": lax.rem(li + nl - 1, nl)}
    right = {"lon": lax.rem(li + 1, nl)}

    def remote(src, dst, sems, i, device):
        return pltpu.make_async_remote_copy(
            src_ref=src, dst_ref=dst, send_sem=sems.at[0, i], recv_sem=sems.at[1, i],
            device_id=device, device_id_type=MESH,
        )

    small = [
        pltpu.make_async_copy(src, dst, load_sem.at[1 + i])
        for i, (src, dst) in enumerate(
            (
                (near_h, near_t), (counts_h, counts), (weight_h, weight_t), (zones_h, zones),
                (owners_h, owners), (rates_h, rates), (reaction_h, reaction),
            )
        )
    ]
    for copy in small[:3]:
        copy.start()
    load = pltpu.make_async_copy(conc, xf, load_sem.at[0])
    load.start()
    for copy in small[3:]:
        copy.start()
    barrier = pltpu.get_barrier_semaphore()
    for device in (left, right):
        pl.semaphore_signal(barrier, inc=1, device_id=device, device_id_type=MESH)
    for d in range(1, nb):

        @pl.when(bi + d < nb)
        def _():
            pl.semaphore_signal(barrier, inc=1, device_id={"bal": bi + d}, device_id_type=MESH)


    for copy in small[:3]:
        copy.wait()
    near = near_t[...]
    band = near // (nblk * nb)
    apart = band - li
    place = jnp.where(
        apart == 0, nblk, jnp.where((apart == 1) | (apart == 1 - nl), 2 * nblk, 0)
    ) + near % nblk
    used = iota((kadj, nblk), 0) < counts[...]
    coef = jnp.where(used, weight_t[...].astype(F32) / 128.0, 0.0)
    which = iota((3 * nblk, nblk), 0)
    ft = jnp.zeros((3 * nblk, nblk), F32)
    for k in range(kadj):
        ft = ft + jnp.where(place[k : k + 1, :] == which, coef[k : k + 1, :], 0.0)
    f_send[...] = jnp.zeros_like(f_send)
    f_send[0, :, :nblk] = ft[:nblk]
    f_send[1, :, :nblk] = ft[2 * nblk :]

    load.wait()
    for h, packed in enumerate(cross(xf[:, :hb, :], xf[:, hb:, :])):
        xp[h] = packed
        xb[h, nblk : 2 * nblk] = packed.astype(BF16)
    pl.semaphore_wait(barrier, 2 + bi)
    to_left = remote(f_send.at[0], f_recv.at[1], f_sems, 0, left)
    to_right = remote(f_send.at[1], f_recv.at[0], f_sems, 1, right)
    to_left.start()
    to_right.start()
    halos = []
    for h in range(2):
        own_blocks = xb.at[h, pl.ds(nblk, nblk)]
        pair_of = (
            remote(own_blocks, xb.at[h, pl.ds(2 * nblk, nblk)], halo_sems, 2 * h, left),
            remote(own_blocks, xb.at[h, pl.ds(0, nblk)], halo_sems, 2 * h + 1, right),
        )
        for copy in pair_of:
            copy.start()
        halos.append(pair_of)

    for d in range(1, nb):

        @pl.when(bi - d >= 0)
        def _():
            pl.semaphore_signal(ready, inc=1, device_id={"bal": bi - d}, device_id_type=MESH)

    for copy in small[3:]:
        copy.wait()
    chem_w[...] = jnp.zeros_like(chem_w)
    chem_w[:width, :width] = reaction[...]
    chem_w[width:, width:] = reaction[...]

    own = owners[...]
    member = jnp.concatenate([(own == o).astype(F32) for o in range(nb)], axis=0)
    member_b = member.astype(BF16)
    before = (iota((blk, blk), 0) < iota((blk, blk), 1)).astype(F32).astype(BF16)
    in_row = dot(member_b, before)
    totals = dot(member_b, jnp.ones((blk, blk), BF16))
    r0, r1 = iota((nb * nblk, nb * nblk), 0), iota((nb * nblk, nb * nblk), 1)
    earlier = ((r0 // nblk == r1 // nblk) & (r1 < r0)).astype(F32).astype(BF16)
    offset = dot(earlier, totals.astype(BF16))
    ranks = (member * (in_row + offset)).reshape(nb, nblk, blk).sum(axis=0)
    slot = own * cap + ranks.astype(jnp.int32)

    table = jnp.exp(-rates[...])
    high = table.astype(BF16)
    rest = table - high.astype(F32)
    mid = rest.astype(BF16)
    low = (rest - mid.astype(F32)).astype(BF16)
    parts = jnp.concatenate([high, mid, low, jnp.zeros_like(low)], axis=0)
    zone_t = zones[...].astype(F32).T.astype(jnp.int32)
    lane = iota((blk, 4 * nzones), 1) % nzones
    for b in range(nblk):
        pick = (zone_t[:, b : b + 1] == lane).astype(F32).astype(BF16)
        rate = dot(pick, parts)
        for h, packed in enumerate(cross(rate[:hb], rate[hb:])):
            factor[h, b] = packed

    spread = (iota((nblk * grp, nblk), 0) // grp == iota((nblk * grp, nblk), 1)).astype(F32)
    spread_b = spread.astype(BF16)
    widen = (iota((nblk, nblk * grp), 1) // grp == iota((nblk, nblk * grp), 0)).astype(F32).astype(BF16)
    same = (
        iota((nblk * grp, nblk * grp), 0) % grp == iota((nblk * grp, nblk * grp), 1) % grp
    ).astype(F32)
    ft_b = ft.astype(BF16)
    to_left.wait_recv()
    to_right.wait_recv()
    from_left = f_recv[0, :, :nblk].astype(BF16)
    from_right = f_recv[1, :, :nblk].astype(BF16)
    own_ft = ft_b[nblk : 2 * nblk]
    a_own = (dot(spread_b, own_ft) + dot_nt(spread_b, own_ft)) * (1.0 - spread)
    a_left = dot_nt(spread_b, ft_b[:nblk]) + dot(spread_b, from_left)
    a_right = dot_nt(spread_b, ft_b[2 * nblk :]) + dot(spread_b, from_right)
    keep = 1.0 - jnp.sum(a_own + a_left + a_right, axis=1, keepdims=True)
    mix_own = (dot(a_own.astype(BF16), widen) * same).astype(BF16)
    for i, a in enumerate((a_left, a_right)):
        mix[:, i * nblk * grp : (i + 1) * nblk * grp] = (dot(a.astype(BF16), widen) * same).astype(BF16)

    def pair(ref, first, j):
        parts = [
            ref[first : first + nblk, g * grp : (g + 1) * grp, :].reshape(nblk * grp, width)
            for g in (j, j + 1)
        ]
        return jnp.concatenate(parts, axis=1)

    def put_pair(ref, j, value):
        for g in (j, j + 1):
            part = value[:, (g - j) * width : (g - j + 1) * width]
            ref[:, g * grp : (g + 1) * grp, :] = part.reshape(nblk, grp, width)

    for h in range(2):
        for j in range(0, hb // grp, 2):
            own_x = xp.at[h]
            put_pair(own_x, j, pair(own_x, 0, j) * keep + dot(mix_own, pair(xb.at[h], nblk, j)))

    slot_row = iota((cap, blk), 0)

    def choose(owner):
        row = slot_row + owner * cap
        return jnp.concatenate(
            [(slot[b : b + 1, :] == row).astype(F32).astype(BF16) for b in range(nblk)], axis=1
        )

    def pick_slots(values, owner):
        return dot(choose(owner), values).astype(BF16)

    def finish(h):
        for copy in halos[h]:
            copy.wait_recv()
        for j in range(0, hb // grp, 2):
            halo = jnp.concatenate([pair(xb.at[h], 0, j), pair(xb.at[h], 2 * nblk, j)], axis=0)
            photo = (pair(xp.at[h], 0, j) + dot(mix[...], halo)) * pair(factor.at[h], 0, j)
            put_pair(xp.at[h], j, photo.astype(BF16).astype(F32))

    def slots_from(source):
        return out_slots.at[pl.ds(pl.multiple_of(source * cap, cap), cap)]

    copies = []

    def send(src, dst, owner):
        copy = remote(src, dst, slot_sems, len(copies), {"bal": owner})
        copy.start()
        copies.append(copy)

    half = nb // 2
    side, place_in = bi // half, lax.rem(bi, half)
    across = [(1 - side) * half + lax.rem(place_in + k, half) for k in range(half)]
    within = [side * half + lax.rem(place_in + k, half) for k in range(1, half)]

    early = raw.shape[0]
    chosen = [choose(across[k]) for k in range(early)]
    finish(0)
    start[:, :hb, :], start[:, hb:, :] = (v.astype(BF16) for v in cross(xp[0], xp[0]))

    def send_half(k, h):
        picked = dot(chosen[k], start[...].reshape(rows, width))
        ahead[k, h] = cross(picked[: cap // 2], picked[cap // 2 :])[h].astype(BF16)
        if k + h == 0:

            @pl.when(bi < nb - 1)
            def _():
                pl.semaphore_wait(ready, nb - 1 - bi)

        send(ahead.at[k, h], raw.at[k, h], across[k])

    for k in range(early):
        send_half(k, 0)
    finish(1)
    start[:, :hb, :], start[:, hb:, :] = (v.astype(BF16) for v in cross(xp[0], xp[1]))
    for k in range(early):
        send_half(k, 1)
    initial = start[...].reshape(rows, width)
    result[...] = chemistry(initial, chem_w[...])
    save = pltpu.make_async_copy(result, out_conc, store_sem.at[0])
    save.start()
    final = result[...]
    for k, owner in enumerate(across[early:] + within, early):
        staged[1 + k] = pick_slots(final, owner)
        send(staged.at[1 + k], slots_from(bi), owner)
    staged[0] = pick_slots(final, bi)
    stores = [save, pltpu.make_async_copy(staged.at[0], slots_from(bi), store_sem.at[1])]
    stores[-1].start()
    for k in range(early):
        for h in range(2):
            copies[k + h * early].wait()
        arrived = jnp.concatenate(cross(raw[k, 0].astype(F32), raw[k, 1].astype(F32)), axis=0)
        staged[1 + k] = chemistry(arrived.astype(BF16), chem_w[...])
        source = (1 - side) * half + lax.rem(place_in + half - k, half)
        stores.append(pltpu.make_async_copy(staged.at[1 + k], slots_from(source), store_sem.at[2 + k]))
        stores[-1].start()
    for copy in (to_left, to_right) + halos[0] + halos[1]:
        copy.wait_send()
    for copy in copies[2 * early :] + stores:
        copy.wait()


def save_kernel(pieces, conc_ref, slots_ref, out_conc, out_slots, sems):
    copies = []
    for src, dst in ((slots_ref, out_slots), (conc_ref, out_conc)):
        part = src.shape[0] // pieces
        for p in range(pieces):
            at = pl.ds(p * part, part)
            copies.append(pltpu.make_async_copy(src.at[at], dst.at[at], sems.at[len(copies)]))
            copies[-1].start()
    for copy in copies:
        copy.wait()


def solution(mesh):
    nl, nb = mesh.shape["lon"], mesh.shape["bal"]
    early = min(2, nb // 2)

    def shards(conc, neighbours, counts, weights, zones, owners, rate_table, reaction):
        rows, width = conc.shape
        nblk = neighbours.shape[0]
        blk = rows // nblk
        cap = 2 * rows // nb
        hbm = pl.BlockSpec(memory_space=pltpu.HBM)
        out_shape = (
            jax.ShapeDtypeStruct((rows, width), BF16),
            jax.ShapeDtypeStruct((nb * cap, width), BF16),
        )
        params = dict(has_side_effects=True, vmem_limit_bytes=48 << 20)
        done = pl.pallas_call(
            functools.partial(step_kernel, nl, nb),
            out_shape=out_shape,
            in_specs=[hbm] * 8,
            out_specs=(pl.BlockSpec(memory_space=pl.ANY),) * 2,
            scratch_shapes=[
                pltpu.VMEM((neighbours.shape[1], nblk), jnp.int32),
                pltpu.VMEM((1, nblk), jnp.int32),
                pltpu.VMEM((neighbours.shape[1], nblk), jnp.int32),
                pltpu.VMEM((nblk, blk), jnp.int32),
                pltpu.VMEM((nblk, blk), jnp.int32),
                pltpu.VMEM(rate_table.shape, F32),
                pltpu.VMEM(reaction.shape, BF16),
                pltpu.VMEM((nblk, blk, width), F32),
                pltpu.VMEM((2, nblk, blk // 2, width), F32),
                pltpu.VMEM((2, 3 * nblk, blk // 2, width), BF16),
                pltpu.VMEM((2, nblk, blk // 2, width), F32),
                pltpu.VMEM((nblk, blk, width), BF16),
                pltpu.VMEM((rows, width), BF16),
                pltpu.VMEM((nb, cap, width), BF16),
                pltpu.VMEM((early, 2, cap // 2, width), BF16),
                pltpu.VMEM((early, 2, cap // 2, width), BF16),
                pltpu.VMEM((2, nblk, 128), F32),
                pltpu.VMEM((2, nblk, 128), F32),
                pltpu.VMEM((nblk * 16, 2 * nblk * 16), BF16),
                pltpu.VMEM((2 * width, 2 * width), BF16),
                pltpu.SemaphoreType.DMA((8,)),
                pltpu.SemaphoreType.DMA((2 + early,)),
                pltpu.SemaphoreType.DMA((2, 2)),
                pltpu.SemaphoreType.DMA((2, 4)),
                pltpu.SemaphoreType.DMA((2, nb - 1 + early)),
                pltpu.SemaphoreType.REGULAR,
            ],
            compiler_params=pltpu.CompilerParams(collective_id=0, **params),
        )(
            *(
                pltpu.with_memory_space_constraint(a, pltpu.HBM)
                for a in (
                    conc.reshape(nblk, blk, width),
                    neighbours.T,
                    counts.reshape(1, nblk),
                    weights.T,
                    zones.reshape(nblk, blk),
                    owners.reshape(nblk, blk),
                    rate_table,
                    reaction,
                )
            )
        )
        pieces = 4
        return pl.pallas_call(
            functools.partial(save_kernel, pieces),
            out_shape=out_shape,
            in_specs=[pl.BlockSpec(memory_space=pl.ANY)] * 2,
            out_specs=(hbm, hbm),
            scratch_shapes=[pltpu.SemaphoreType.DMA((2 * pieces,))],
            compiler_params=pltpu.CompilerParams(**params),
        )(*done)

    in_specs = (
        P(("lon", "bal"), None),
        P(("lon", "bal"), None),
        P(("lon", "bal")),
        P(("lon", "bal"), None),
        P(("lon", "bal")),
        P(("lon", "bal"), None),
        P(),
        P(),
    )
    out_specs = (P(("lon", "bal"), None), P(("lon", "bal"), None))
    return jax.shard_map(shards, mesh=mesh, in_specs=in_specs, out_specs=out_specs, check_vma=False)
```
